32 devices in a mesh: batch: 8 (over z, core), vocab: 4 (over y, x).
Axes of the slice: x: 2, y: 2, z: 4, core: 2. Of those that a mesh axis runs over, the one named last changes fastest.
Arguments:
- hidden: bfloat16 [1024, 4096], P('batch'), may hold values from -40 to 40
- exit_layer: int32 [1024], P('batch'), may hold values from 0 to 7
- exit_gains: float32 [8, 4096], replicated, may hold values from 0.1 to 1.9
- unembed: bfloat16 [4096, 128256], P(None, ('batch', 'vocab')), may hold values from -10 to 10
- targets: int32 [1024], replicated, may hold values from 0 to 128255
- values: float32 [1024], P('batch'), may hold values from -6 to 6
- rewards: float32 [1024], P('batch'), may hold values from -2 to 2
- ref_logprob: float32 [1024], P('batch'), may hold values from -16 to -6
- segment_end: int32 [1024], P('batch'), may hold values 0 or 1
Outputs:
- logprob: float32 [1024], P('batch')
- advantages: float32 [1024], P('batch')
The draws below stay inside these ranges and needn't reach their ends.
All inputs are finite; a program needn't handle non-finite values. No bound on the sum of `segment_end` on one device may be relied on, other than what follows from the above.
Results may differ from the reference program's by a relative error of at most 0.00054.
Values may be sent and summed in bfloat16 or wider, within the bound.
No kernel may reach another device: no remote copies, remote signals or barrier semaphores. Data moves between devices by JAX's collectives and lax.ppermute only.
A program may use at most 128 MiB of HBM per device.

```python
import math
import jax
import jax.numpy as jnp
import numpy as np
from jax import lax

D = 4096
VOCAB = 128256
EXITS = 8
TOK_B = 128
TOKENS = 1024


def draw_hidden(key, part):
    keys = jax.random.split(jax.random.fold_in(key, 1), 3)
    base = jnp.clip(jax.random.normal(keys[0], (TOKENS, D), jnp.float32), -4.0, 4.0)
    row_scale = jnp.exp(jax.random.uniform(keys[1], (TOKENS, 1), jnp.float32) * jnp.log(10.0))
    col_scale = jnp.exp(jax.random.uniform(keys[2], (1, D), jnp.float32) * jnp.log(10.0))
    result = base * row_scale * col_scale / 10.0
    return result.astype(jnp.bfloat16)


def draw_unembed(key, part):
    base = jnp.clip(jax.random.normal(jax.random.fold_in(key, 2), (D, VOCAB), jnp.float32), -4.0, 4.0)
    result = base * (3.0 / jnp.sqrt(jnp.float32(D)))
    return result.astype(jnp.bfloat16)


def with_ends(values, stream_key, smallest, top_value):
    shape = values.shape
    place = [jax.random.randint(jax.random.fold_in(stream_key, axis), (), 0, shape[axis]) for axis in range(len(shape))]
    values = values.at[tuple(place)].set(smallest)
    longest = shape.index(max(shape))
    place[longest] = (place[longest] + 1) % shape[longest]
    return values.at[tuple(place)].set(top_value)


def shard_levels(stream_key, extent, pieces, least, high):
    gain, own = 1.0, jax.random.fold_in(stream_key, 6)
    for position, blocks in pieces:
        steps = jnp.exp(jax.random.uniform(jax.random.fold_in(own, position), (blocks,), jnp.float32, least / len(pieces), high / len(pieces)))
        gain = gain * jnp.repeat(steps, extent[position] // blocks).reshape([-1 if axis == position else 1 for axis in range(len(extent))])
    return gain


def ranked_wide(stream_key, extent, count, lean):
    portions = [min(1 << octave, count + 1 - (1 << octave)) * (1 << 20) // math.isqrt((1 << octave) ** lean) + 1 for octave in range((count + 1).bit_length()) if 1 << octave <= count]
    spread = 1 + sum(portions) // (1 << 30)
    table = np.cumsum(np.array([max(1, weight // spread) for weight in portions]))
    pick = jax.random.randint(jax.random.fold_in(stream_key, 1), extent, 0, int(table[len(portions) - 1]))
    start = jnp.left_shift(1, jnp.searchsorted(jnp.asarray(table, jnp.int32), pick, side="right").astype(jnp.int32))
    grade = start - 1 + jax.random.randint(jax.random.fold_in(stream_key, 4), extent, 0, 1 << 30) % jnp.minimum(start, count + 1 - start)
    return jax.random.permutation(jax.random.fold_in(stream_key, 2), count)[grade].astype(jnp.int32)


def gaussian(own_key, shape, deviation, reach, pieces=(), held_as=jnp.bfloat16):
    drawn = deviation * jax.random.normal(own_key, shape, jnp.float32)
    if pieces:
        drawn = drawn * shard_levels(own_key, shape, pieces, -0.22, 0.18)
    return jnp.clip(drawn, -reach, reach).astype(held_as)


def setup_inputs(seed: int = 0) -> dict:
    splits = jax.random.split(jax.random.key(seed), 10)
    return {
        "hidden": draw_hidden(jax.random.fold_in(splits[9], 71), 0),
        "exit_layer": with_ends(jax.random.randint(splits[1], (TOKENS,), 0, EXITS), jax.random.fold_in(splits[1], 1), 0, EXITS - 1).astype(jnp.int32),
        "exit_gains": jnp.clip(1.0 + 0.18 * jax.random.normal(splits[2], (EXITS, D), jnp.float32), 0.1, 1.9),
        "unembed": draw_unembed(jax.random.fold_in(splits[9], 71), 0),
        "targets": with_ends(ranked_wide(splits[4], (TOKENS,), VOCAB, 2), jax.random.fold_in(splits[4], 3), 0, VOCAB - 1).astype(jnp.int32),
        "values": gaussian(splits[5], (TOKENS,), 1.0, 6.0, ((0, 8),), jnp.float32),
        "rewards": gaussian(splits[6], (TOKENS,), 0.3, 2.0, ((0, 8),), jnp.float32),
        "ref_logprob": jnp.clip(-16.0 + 10.0 * jax.random.uniform(splits[7], (TOKENS,), jnp.float32) ** shard_levels(splits[7], (TOKENS,), ((0, 8),), -0.2, 0.2), -16.0, -6.0),
        "segment_end": with_ends((jax.random.randint(splits[8], (TOKENS,), 0, 4 * TOK_B) < 1).astype(jnp.int32), jax.random.fold_in(splits[8], 1), 0, 1),
    }


epsilon_norm = 1e-05
discount = 1.0
trace_decay = 0.999
penalty_weight = 0.1

def reference(hidden, exit_layer, exit_gains, unembed, targets, values, rewards, ref_logprob, segment_end):
    states = hidden.astype(jnp.float32)
    inverse = lax.rsqrt(lax.optimization_barrier(jnp.mean(states * states, axis=-1, keepdims=True)) + epsilon_norm)
    normed = (states * inverse * exit_gains[exit_layer]).astype(jnp.bfloat16)
    weight_wide = unembed.astype(jnp.float32)

    def score_block(pair):
        block_rows, block_ids = pair
        logits = jnp.dot(block_rows.astype(jnp.float32), weight_wide, precision=lax.Precision.HIGHEST)
        row_max = lax.optimization_barrier(jnp.max(logits, axis=1))
        row_total = lax.optimization_barrier(jnp.sum(jnp.exp(logits - row_max[:, None]), axis=1))
        picked = jnp.take_along_axis(logits, block_ids[:, None], axis=1)[:, 0]
        return picked - (row_max + jnp.log(row_total))
    blocks = TOKENS // TOK_B
    logprob = lax.map(score_block, (normed.reshape(blocks, TOK_B, D), targets.reshape(blocks, TOK_B))).reshape(TOKENS)
    keeping = 1.0 - segment_end.astype(jnp.float32)
    next_values = jnp.concatenate([values[1:], jnp.zeros((1,), jnp.float32)])
    shaped = rewards - penalty_weight * (logprob - ref_logprob)
    deltas = shaped + discount * next_values * keeping - values
    factors = discount * trace_decay * keeping

    def backward(running, inputs):
        factor, delta = inputs
        running = delta + factor * running
        return (running, running)
    finished, advantages = lax.scan(backward, jnp.zeros((), jnp.float32), (factors, deltas), reverse=True)
    return (logprob, advantages)
```

```python
import math

import jax
import jax.numpy as jnp
from jax import lax
from jax.experimental import pallas as pl
from jax.experimental.pallas import tpu as pltpu
from jax.sharding import PartitionSpec as P

epsilon_norm = 1e-05
discount = 1.0
trace_decay = 0.999
penalty_weight = 0.1
CORES = 2
LOWEST = float(jnp.finfo(jnp.float32).min)
VMEM = pl.BlockSpec(memory_space=pltpu.VMEM)
ANY = pl.BlockSpec(memory_space=pl.ANY)
HBM = pl.BlockSpec(memory_space=pltpu.HBM)
RESIDENT = True
MIB = 2**20


class Grid:
    def __init__(self, mesh):
        self.peers, self.groups = mesh.shape["batch"], mesh.shape["vocab"]
        self.planes = self.peers // CORES
        self.side = math.isqrt(self.groups)

    def moves(self, target):
        pairs = []
        for b in range(self.peers):
            for v in range(self.groups):
                z, c, y, x = target(b // CORES, b % CORES, v // self.side, v % self.side)
                pairs.append((b * self.groups + v, (z * CORES + c) * self.groups + y * self.side + x))
        return pairs

    def send(self, array, target):
        return lax.ppermute(array, ("batch", "vocab"), self.moves(target))

    def twin(self, array):
        return self.send(array, lambda z, c, y, x: (z, 1 - c, y, x))

    def up(self, array):
        return self.send(array, lambda z, c, y, x: ((z + 1) % self.planes, c, y, x))

    def along_x(self, array):
        return self.send(array, lambda z, c, y, x: (z, c, y, x ^ 1))

    def along_y(self, array):
        return self.send(array, lambda z, c, y, x: (z, c, y ^ 1, x))

    def place(self):
        b, v = lax.axis_index("batch"), lax.axis_index("vocab")
        half = lax.rem(lax.div(v, self.side) + lax.rem(v, self.side), 2)
        return lax.div(b, CORES), lax.rem(b, CORES), half


def normalize_kernel(grid, hidden_ref, layers_ref, gains_ref, out_ref, half_ref):
    rows = hidden_ref.shape[0]
    block = 16
    exits = gains_ref.shape[0]
    layers = jnp.broadcast_to(layers_ref[...], (rows, rows)).astype(jnp.float32).T
    for begin in range(0, rows, block):
        part = pl.ds(begin, block)
        states = hidden_ref[part, :].astype(jnp.float32)
        mean = jnp.sum(states * states, axis=1, keepdims=True) / states.shape[1]
        inverse = lax.rsqrt(mean + epsilon_norm)
        layer = layers[begin : begin + block, :1]
        scaling = jnp.broadcast_to(gains_ref[0:1, :], states.shape)
        for index in range(1, exits):
            scaling = jnp.where(layer == float(index), gains_ref[index : index + 1, :], scaling)
        out_ref[part, :] = (states * inverse * scaling).astype(out_ref.dtype)
    half = grid.place()[2]
    length = rows // 2
    half_ref[...] = out_ref[pl.ds(pl.multiple_of(half * length, length), length), :]


def spans(rows, target):
    count = max(1, round(rows / target))
    size = -(-rows // (count * 16)) * 16
    return [(begin, min(size, rows - begin)) for begin in range(0, rows, size)]


def tally(logits, begin, wanted, carry):
    old, total, pick = carry
    place = lax.broadcasted_iota(jnp.int32, logits.shape, 0) + begin
    new = jnp.maximum(old, jnp.max(logits, axis=0, keepdims=True))
    total = total * jnp.exp(old - new) + jnp.sum(jnp.exp(logits - new), axis=0, keepdims=True)
    pick = pick + jnp.sum(jnp.where(place == wanted, logits, 0.0), axis=0, keepdims=True)
    return new, total, pick


def product(weights, states):
    return lax.dot_general(
        weights, states, (((1,), (1,)), ((), ())), preferred_element_type=jnp.float32
    )


def score_kernel(grid, step, pieces, first, last, *refs):
    refs = list(refs)
    ids_ref, weights_in = refs.pop(0), refs.pop(0)
    parts_in = None if first else refs.pop(0)
    values_ref = refs.pop(0) if last else None
    piece_refs = [refs.pop(0) for _ in pieces]
    parts_ref = refs.pop(0)
    weights_ref = weights_in
    states_ref, piece_sem = refs.pop(0), refs.pop(0)
    rows = weights_ref.shape[0]
    plane, core, half = grid.place()
    source = lax.rem(plane - step + grid.planes, grid.planes)
    copies = []
    for index, (piece, ref) in enumerate(zip(pieces, piece_refs)):
        offset = pl.multiple_of(piece(core, half), ref.shape[0])
        copies.append(
            pltpu.make_async_copy(ref, states_ref.at[pl.ds(offset, ref.shape[0])], piece_sem.at[index])
        )
    for copy in copies:
        copy.start()
    blocks = spans(rows, 1336)
    fetches = []
    for copy in copies:
        copy.wait()
    start = (lax.axis_index("batch") * grid.groups + lax.axis_index("vocab")) * rows
    wanted = ids_ref[source] - start
    tokens = states_ref.shape[0]
    carry = (
        jnp.full((1, tokens), LOWEST, jnp.float32),
        jnp.zeros((1, tokens), jnp.float32),
        jnp.zeros((1, tokens), jnp.float32),
    )
    pending = None
    for index, (begin, size) in enumerate(blocks):
        logits = product(weights_ref[begin : begin + size, :], states_ref[...])
        if pending is not None:
            carry = tally(*pending, wanted, carry)
        pending = (logits, begin)
    carry = tally(*pending, wanted, carry)
    owned = tokens // CORES
    if not last:
        if not first:
            parts_ref[...] = parts_in[...]
        for index in range(3):
            parts_ref[source, index : index + 1, :] = carry[index]
        return
    for group in range(grid.planes):
        here = source == group
        for index in range(4):
            if index < 3:
                row = jnp.where(here, carry[index], parts_in[group, index : index + 1, :])
            else:
                row = jnp.broadcast_to(values_ref[0:1, 0:1], (1, tokens))
            for side in range(CORES):
                part = row[:, side * owned : (side + 1) * owned]
                for column in range(grid.groups):
                    parts_ref[(group * CORES + side) * grid.groups + column, index : index + 1, :] = part


def score(grid, step, pieces, ids, weights, parts, values, first, last):
    owned = pieces[0][1].shape[0] if first else pieces[0][1].shape[0] * 2
    width = weights.shape[1]
    rows = weights.shape[0]
    tokens = owned * CORES
    if last:
        out_shape = jax.ShapeDtypeStruct((grid.peers * grid.groups, 4, owned), jnp.float32)
    else:
        out_shape = jax.ShapeDtypeStruct((grid.planes, 3, tokens), jnp.float32)
    args = [ids, weights]
    specs = [VMEM, VMEM]
    if not first:
        args.append(parts)
        specs.append(VMEM)
    if last:
        args.append(values)
        specs.append(VMEM)
    args += [array for _, array in pieces]
    specs += [HBM] * len(pieces)
    scratch = [
        pltpu.VMEM((tokens, width), jnp.bfloat16),
        pltpu.SemaphoreType.DMA((len(pieces),)),
    ]
    out_specs = VMEM
    limit = 8
    offsets = [offset for offset, _ in pieces]
    return pl.pallas_call(
        lambda *refs: score_kernel(grid, step, offsets, first, last, *refs),
        out_shape=out_shape,
        in_specs=specs,
        out_specs=out_specs,
        scratch_shapes=scratch,
        compiler_params=pltpu.CompilerParams(vmem_limit_bytes=limit * MIB),
        cost_estimate=pl.CostEstimate(
            flops=2 * rows * tokens * width, transcendentals=rows * tokens, bytes_accessed=0
        ),
        name=f"score{step}",
    )(*args)


def load_kernel(weights_in, weights_ref, sem):
    copy = pltpu.make_async_copy(weights_in, weights_ref, sem)
    copy.start()
    copy.wait()


def tail_kernel(grid, parts_ref, values_ref, rewards_ref, anchor_ref, ends_ref,
                logprob_ref, heads_ref, accrued_ref, product_ref):
    here = lax.axis_index("batch")
    peers = grid.peers
    owned = values_ref.shape[1]
    maxima = parts_ref[:, 0, :]
    larger = jnp.max(maxima, axis=0, keepdims=True)
    total = jnp.sum(parts_ref[:, 1, :] * jnp.exp(maxima - larger), axis=0, keepdims=True)
    picked = jnp.sum(parts_ref[:, 2, :], axis=0, keepdims=True)
    logprob = picked - (larger + jnp.log(total))
    logprob_ref[...] = logprob
    place = lax.broadcasted_iota(jnp.int32, (8, owned), 1)

    def wide(row):
        return jnp.broadcast_to(row, (8, owned))

    def ahead(array, steps):
        return pltpu.roll(array, owned - steps, 1)

    behind = jnp.minimum(here + 1, peers - 1)
    entering = wide(parts_ref[pl.ds(behind * grid.groups, 1), 3, :])
    entering = jnp.where(here + 1 < peers, entering, 0.0)
    values = wide(values_ref[...])
    following = jnp.where(place < owned - 1, ahead(values, 1), entering)
    keeping = 1.0 - wide(ends_ref[...]).astype(jnp.float32)
    shaped = wide(rewards_ref[...]) - penalty_weight * (wide(logprob) - wide(anchor_ref[...]))
    accrued = shaped + discount * following * keeping - values
    product = discount * trace_decay * keeping
    steps = 1
    while steps < owned:
        inside = place < owned - steps
        accrued = accrued + product * jnp.where(inside, ahead(accrued, steps), 0.0)
        product = product * jnp.where(inside, ahead(product, steps), 1.0)
        steps *= 2
    accrued_ref[...] = accrued[:1]
    product_ref[...] = product[:1]
    for index in range(peers):
        heads_ref[index, 0:1, :] = jnp.broadcast_to(accrued[:1, :1], (1, owned))
        heads_ref[index, 1:2, :] = jnp.broadcast_to(product[:1, :1], (1, owned))


def finish_kernel(heads_ref, accrued_ref, product_ref, out_ref):
    here = lax.axis_index("batch")
    incoming = jnp.zeros((1, heads_ref.shape[2]), jnp.float32)
    for source in range(heads_ref.shape[0] - 1, 0, -1):
        passed = heads_ref[source, 0:1, :] + heads_ref[source, 1:2, :] * incoming
        incoming = jnp.where(source > here, passed, incoming)
    out_ref[...] = accrued_ref[...] + product_ref[...] * incoming


def finish(grid, parts, values, rewards, ref_logprob, segment_end):
    owned = values.shape[1]
    parts = lax.all_to_all(parts, ("batch", "vocab"), split_axis=0, concat_axis=0, tiled=True)
    row = jax.ShapeDtypeStruct((1, owned), jnp.float32)
    heads = jax.ShapeDtypeStruct((grid.peers, 2, owned), jnp.float32)
    logprob, heads, accrued, product = pl.pallas_call(
        lambda *refs: tail_kernel(grid, *refs),
        out_shape=(row, heads, row, row),
        in_specs=[VMEM] * 5,
        out_specs=(VMEM,) * 4,
        name="tail",
    )(parts, values, rewards, ref_logprob, segment_end)
    heads = lax.all_to_all(heads, "batch", split_axis=0, concat_axis=0, tiled=True)
    advantages = pl.pallas_call(
        finish_kernel,
        out_shape=row,
        in_specs=[VMEM] * 3,
        out_specs=VMEM,
        name="finish",
    )(heads, accrued, product)
    return logprob[0], advantages[0]


def per_device(
    grid, hidden, exit_layer, exit_gains, unembed, targets, values, rewards, ref_logprob, segment_end
):
    owned, width = hidden.shape
    half_rows = owned // 2
    normed, held = pl.pallas_call(
        lambda *refs: normalize_kernel(grid, *refs),
        out_shape=(
            jax.ShapeDtypeStruct((owned, width), jnp.bfloat16),
            jax.ShapeDtypeStruct((half_rows, width), jnp.bfloat16),
        ),
        in_specs=[VMEM] * 3,
        out_specs=(VMEM, VMEM),
        compiler_params=pltpu.CompilerParams(vmem_limit_bytes=16*MIB),
        name="normalize",
    )(hidden, exit_layer[None], exit_gains)
    ids = targets.reshape(grid.planes, 1, CORES * owned)
    weights = pl.pallas_call(
        load_kernel,
        out_shape=pltpu.VMEM(unembed.T.shape, unembed.dtype),
        in_specs=[ANY],
        out_specs=VMEM,
        scratch_shapes=[pltpu.SemaphoreType.DMA],
        compiler_params=pltpu.CompilerParams(vmem_limit_bytes=2 * MIB),
        name="load",
    )(unembed.T)
    parts = None
    values = values[None]
    twin = grid.twin(normed)
    above, other = grid.up(held), None
    for step in range(grid.planes):
        if step == 0:
            pieces = [
                (lambda core, half: core * owned, normed),
                (lambda core, half: (1 - core) * owned, twin),
            ]
            ahead, weights = lax.optimization_barrier((above, weights))
        else:
            other, parts = lax.optimization_barrier((other, parts))
            pieces = [
                (lambda core, half: core * owned + half * half_rows, held),
                (lambda core, half: core * owned + (1 - half) * half_rows, other),
                (lambda core, half: (1 - core) * owned + half * half_rows, twin),
                (lambda core, half: (1 - core) * owned + (1 - half) * half_rows, grid.twin(other)),
            ]
            if step + 1 < grid.planes:
                ahead, parts = lax.optimization_barrier((above, parts))
        if step + 1 < grid.planes:
            held = ahead
            other = grid.along_y(held) if step % 2 else grid.along_x(held)
            twin = grid.twin(held)
            if step + 2 < grid.planes:
                above = grid.up(held)
        first, last = step == 0, step == grid.planes - 1
        result = score(grid, step, pieces, ids, weights, parts, values, first, last)
        parts = result
    return finish(
        grid, parts, values, rewards[None], ref_logprob[None], segment_end[None]
    )


def solution(mesh):
    grid = Grid(mesh)
    placed = (
        P("batch", None),
        P("batch"),
        P(),
        P(None, ("batch", "vocab")),
        P(),
        P("batch"),
        P("batch"),
        P("batch"),
        P("batch"),
    )
    return jax.shard_map(
        lambda *arrays: per_device(grid, *arrays),
        mesh=mesh,
        in_specs=placed,
        out_specs=(P("batch"), P("batch")),
        check_vma=False,
    )
```

```python
import math

import jax
import jax.numpy as jnp
from jax import lax
from jax.experimental import pallas as pl
from jax.experimental.pallas import tpu as pltpu
from jax.sharding import PartitionSpec as P


epsilon_norm = 1e-05
discount = 1.0
trace_decay = 0.999
penalty_weight = 0.1
CORES = 2
LOWEST = float(jnp.finfo(jnp.float32).min)
VMEM = pl.BlockSpec(memory_space=pltpu.VMEM)
ANY = pl.BlockSpec(memory_space=pl.ANY)
HBM = pl.BlockSpec(memory_space=pltpu.HBM)
MIB = 2**20


class Grid:
    def __init__(self, mesh):
        self.peers, self.groups = mesh.shape["batch"], mesh.shape["vocab"]
        self.planes = self.peers // CORES
        self.side = math.isqrt(self.groups)

    def moves(self, target):
        pairs = []
        for b in range(self.peers):
            for v in range(self.groups):
                z, c, y, x = target(b // CORES, b % CORES, v // self.side, v % self.side)
                pairs.append((b * self.groups + v, (z * CORES + c) * self.groups + y * self.side + x))
        return pairs

    def send(self, array, target):
        return lax.ppermute(array, ("batch", "vocab"), self.moves(target))

    def twin(self, array):
        return self.send(array, lambda z, c, y, x: (z, 1 - c, y, x))

    def line(self, position):
        position %= self.planes
        return 2 * position - 1 if 0 < 2 * position <= self.planes else 2 * (self.planes - position) % self.planes

    def up(self, array, steps=1):
        where = {self.line(position): position for position in range(self.planes)}
        return self.send(array, lambda z, c, y, x: (self.line(where[z] + steps), c, y, x))

    def origin(self, plane, steps):
        if steps == 0:
            return plane
        count = self.planes
        even = lax.rem(count - lax.div(plane, 2), count)
        position = jnp.where(lax.rem(plane, 2) == 1, lax.div(plane + 1, 2), even)
        position = lax.rem(position - steps + count, count)
        low = (position > 0) & (2 * position <= count)
        return jnp.where(low, 2 * position - 1, lax.rem(2 * (count - position), count))

    def across(self, array, down, along):
        side = self.side
        return self.send(array, lambda z, c, y, x: (z, c, (y + down) % side, (x + along) % side))

    def along_x(self, array):
        return self.send(array, lambda z, c, y, x: (z, c, y, x ^ 1))

    def along_y(self, array):
        return self.send(array, lambda z, c, y, x: (z, c, y ^ 1, x))

    def place(self):
        b, v = lax.axis_index("batch"), lax.axis_index("vocab")
        half = lax.rem(lax.div(v, self.side) + lax.rem(v, self.side), 2)
        return lax.div(b, CORES), lax.rem(b, CORES), half


def normalize_kernel(grid, halved, hidden_hbm, layers_hbm, gains_hbm, out_ref,
                     states_ref, layers_ref, wide_ref, gains_ref, sem):
    rows = out_ref.shape[0]
    block = 16
    chunk = 32
    exits = gains_ref.shape[0]
    start = pl.multiple_of(grid.place()[2] * rows, rows) if halved else 0
    small = [
        pltpu.make_async_copy(layers_hbm, layers_ref, sem.at[0]),
        pltpu.make_async_copy(gains_hbm, gains_ref, sem.at[1]),
    ]
    large = []
    for index in range(rows // chunk):
        large.append(
            pltpu.make_async_copy(
                hidden_hbm.at[pl.ds(start + index * chunk, chunk)],
                states_ref.at[pl.ds(index * chunk, chunk)],
                sem.at[2 + index],
            )
        )
    for copy in small + large:
        copy.start()
    small[0].wait()
    owned = layers_ref.shape[1]
    wide_ref[...] = jnp.broadcast_to(layers_ref[...], (owned, owned)).astype(jnp.float32).T
    small[1].wait()
    for index, copy in enumerate(large):
        copy.wait()

        def body(turn, carry):
            begin = pl.multiple_of(index * chunk + turn * block, block)
            part = pl.ds(begin, block)
            states = states_ref[part, :].astype(jnp.float32)
            mean = jnp.sum(states * states, axis=1, keepdims=True) / states.shape[1]
            inverse = lax.rsqrt(mean + epsilon_norm)
            layer = wide_ref[pl.ds(pl.multiple_of(start + begin, block), block), :1]
            scaling = jnp.broadcast_to(gains_ref[0:1, :], states.shape)
            for exit_index in range(1, exits):
                scaling = jnp.where(
                    layer == float(exit_index), gains_ref[exit_index : exit_index + 1, :], scaling
                )
            out_ref[part, :] = (states * inverse * scaling).astype(out_ref.dtype)
            return carry

        lax.fori_loop(0, chunk // block, body, 0)


def normalize(grid, halved, hidden, layers, gains):
    owned, width = hidden.shape
    rows = owned // 2 if halved else owned
    return pl.pallas_call(
        lambda *refs: normalize_kernel(grid, halved, *refs),
        out_shape=jax.ShapeDtypeStruct((rows, width), jnp.bfloat16),
        in_specs=[HBM] * 3,
        out_specs=VMEM,
        scratch_shapes=[
            pltpu.VMEM((rows, width), hidden.dtype),
            pltpu.VMEM(layers.shape, layers.dtype),
            pltpu.VMEM((owned, owned), jnp.float32),
            pltpu.VMEM(gains.shape, gains.dtype),
            pltpu.SemaphoreType.DMA((2 + rows // 32,)),
        ],
        compiler_params=pltpu.CompilerParams(vmem_limit_bytes=60 * MIB),
        name="share" if halved else "normalize",
    )(hidden, layers, gains)


def spans(rows, target):
    count = max(1, round(rows / target))
    size = -(-rows // (count * 16)) * 16
    return [(begin, min(size, rows - begin)) for begin in range(0, rows, size)]


def tally(logits, begin, wanted, carry):
    old, total, pick = carry
    place = lax.broadcasted_iota(jnp.int32, logits.shape, 0) + begin
    new = jnp.maximum(old, jnp.max(logits, axis=0, keepdims=True))
    total = total * jnp.exp(old - new) + jnp.sum(jnp.exp(logits - new), axis=0, keepdims=True)
    pick = pick + jnp.sum(jnp.where(place == wanted, logits, 0.0), axis=0, keepdims=True)
    return new, total, pick


def product(weights, states):
    return lax.dot_general(
        weights, states, (((1,), (1,)), ((), ())), preferred_element_type=jnp.float32
    )


def score_kernel(grid, step, pieces, first, *refs):
    refs = list(refs)
    ids_ref, weights_in = refs.pop(0), refs.pop(0)
    parts_in = None if first else refs.pop(0)
    piece_refs = [refs.pop(0) for _ in pieces]
    parts_ref = refs.pop(0)
    weights_ref = weights_in
    states_ref, piece_sem = refs.pop(0), refs.pop(0)
    rows = weights_ref.shape[0]
    plane, core, half = grid.place()
    source = grid.origin(plane, step)
    copies = []
    for index, (piece, ref) in enumerate(zip(pieces, piece_refs)):
        offset = pl.multiple_of(piece(core, half), ref.shape[0])
        copies.append(
            pltpu.make_async_copy(ref, states_ref.at[pl.ds(offset, ref.shape[0])], piece_sem.at[index])
        )
    for copy in copies:
        copy.start()
    blocks = spans(rows, 1336)
    for copy in copies:
        copy.wait()
    start = (lax.axis_index("batch") * grid.groups + lax.axis_index("vocab")) * rows
    wanted = ids_ref[source] - start
    tokens = states_ref.shape[0]
    carry = (
        jnp.full((1, tokens), LOWEST, jnp.float32),
        jnp.zeros((1, tokens), jnp.float32),
        jnp.zeros((1, tokens), jnp.float32),
    )
    pending = None
    for begin, size in blocks:
        logits = product(weights_ref[begin : begin + size, :], states_ref[...])
        if pending is not None:
            carry = tally(*pending, wanted, carry)
        pending = (logits, begin)
    carry = tally(*pending, wanted, carry)
    if not first:
        parts_ref[...] = parts_in[...]
    for index in range(3):
        parts_ref[source, index : index + 1, :] = carry[index]


def score(grid, step, pieces, ids, weights, parts, first):
    owned = pieces[0][1].shape[0] if first else pieces[0][1].shape[0] * 2
    width = weights.shape[1]
    rows = weights.shape[0]
    tokens = owned * CORES
    out_shape = jax.ShapeDtypeStruct((grid.planes, 3, tokens), jnp.float32)
    args = [ids, weights]
    specs = [VMEM, VMEM]
    if not first:
        args.append(parts)
        specs.append(VMEM)
    args += [array for _, array in pieces]
    specs += [HBM] * len(pieces)
    scratch = [
        pltpu.VMEM((tokens, width), jnp.bfloat16),
        pltpu.SemaphoreType.DMA((len(pieces),)),
    ]
    out_specs = VMEM
    limit = 8
    offsets = [offset for offset, _ in pieces]
    return pl.pallas_call(
        lambda *refs: score_kernel(grid, step, offsets, first, *refs),
        out_shape=out_shape,
        in_specs=specs,
        out_specs=out_specs,
        scratch_shapes=scratch,
        compiler_params=pltpu.CompilerParams(vmem_limit_bytes=limit * MIB),
        cost_estimate=pl.CostEstimate(
            flops=2 * rows * tokens * width, transcendentals=rows * tokens, bytes_accessed=0
        ),
    )(*args)


def load_kernel(weights_in, weights_ref, sem):
    copy = pltpu.make_async_copy(weights_in, weights_ref, sem)
    copy.start()
    copy.wait()


def joined(sources):
    larger = sources[0][0]
    for source in sources[1:]:
        larger = jnp.maximum(larger, source[0])
    total = sum(source[1] * jnp.exp(source[0] - larger) for source in sources)
    return larger, total, sum(source[2] for source in sources)


def triple(ref, count):
    return [ref[index * count : (index + 1) * count, :] for index in range(3)]


def brought(kernel, count):
    def body(*refs):
        held, sem = refs[len(refs) - count - 1 : -1], refs[-1]
        copies = [
            pltpu.make_async_copy(ref, to, sem.at[index])
            for index, (ref, to) in enumerate(zip(refs[:count], held))
        ]
        for copy in copies:
            copy.start()
        for copy in copies:
            copy.wait()
        kernel(*held, *refs[count : len(refs) - count - 1])

    return body


def gather_call(kernel, arrays, out_shape, scratch):
    many = isinstance(out_shape, tuple)
    held = [pltpu.VMEM(array.shape, array.dtype) for array in arrays]
    return pl.pallas_call(
        brought(kernel, len(arrays)),
        out_shape=out_shape,
        in_specs=[ANY] * len(arrays),
        out_specs=(VMEM,) * len(out_shape) if many else VMEM,
        scratch_shapes=scratch + held + [pltpu.SemaphoreType.DMA((len(arrays),))],
        compiler_params=pltpu.CompilerParams(vmem_limit_bytes=4 * MIB),
    )(*arrays)


def pack_kernel(grid, *refs):
    parts, rows, out_ref = refs[: grid.groups], refs[grid.groups : -1], refs[-1]
    count = grid.planes
    merged = joined([[ref[:, index, :] for index in range(3)] for ref in parts])
    for index in range(3):
        out_ref[index * count : (index + 1) * count, :] = merged[index]
    tokens = out_ref.shape[1]
    owned = tokens // CORES
    core = grid.place()[1]
    lane = lax.broadcasted_iota(jnp.int32, (1, tokens), 1)
    mine = (lane >= core * owned) & (lane < core * owned + owned)
    for index, ref in enumerate(rows):
        row = ref[...].astype(jnp.float32)
        row = jnp.concatenate([row] * CORES, axis=1)
        out_ref[3 * count + index : 3 * count + index + 1, :] = jnp.where(mine, row, 0.0)


def pair_kernel(grid, mine_ref, other_ref, out_ref):
    count = grid.planes
    merged = joined([triple(mine_ref, count), triple(other_ref, count)])
    for index in range(3):
        out_ref[index * count : (index + 1) * count, :] = merged[index]
    out_ref[3 * count :, :] = mine_ref[3 * count :, :] + other_ref[3 * count :, :]


def tail_kernel(grid, *refs):
    count = grid.planes
    sources = refs[:count]
    logprob_out, advantage_out, rows_ref, logprob_ref, advantage_ref = refs[count:]
    peers, owned = logprob_ref.shape
    plane = grid.place()[0]
    larger, total, picked = joined([triple(ref, count) for ref in sources])
    logprob = picked - (larger + jnp.log(total))
    for group in range(count):
        for core in range(CORES):
            span = slice(core * owned, (core + 1) * owned)
            row = group * CORES + core
            logprob_ref[row : row + 1, :] = logprob[group : group + 1, span]
    for step, ref in enumerate(sources):
        source = grid.origin(plane, step)
        for core in range(CORES):
            span = slice(core * owned, (core + 1) * owned)
            rows_ref[source * CORES + core] = ref[3 * count :, span]
    rows_ref[peers] = jnp.zeros(rows_ref.shape[1:], jnp.float32)
    lane = lax.broadcasted_iota(jnp.int32, (peers, owned), 1)
    line = lax.broadcasted_iota(jnp.int32, (peers, owned), 0)
    logprob = logprob_ref[...]
    values = rows_ref[0:peers, 0, :]
    entering = jnp.broadcast_to(rows_ref[1 : peers + 1, 0, :][:, :1], (peers, owned))
    following = jnp.where(lane < owned - 1, pltpu.roll(values, owned - 1, 1), entering)
    keeping = 1.0 - rows_ref[0:peers, 3, :]
    shaped = rows_ref[0:peers, 1, :] - penalty_weight * (logprob - rows_ref[0:peers, 2, :])
    accrued = shaped + discount * following * keeping - values
    product = discount * trace_decay * keeping

    def doubled(accrued, product, place, extent, axis):
        steps = 1
        while steps < extent:
            inside = place < extent - steps
            later = jnp.where(inside, pltpu.roll(accrued, extent - steps, axis), 0.0)
            accrued = accrued + product * later
            product = product * jnp.where(inside, pltpu.roll(product, extent - steps, axis), 1.0)
            steps *= 2
        return accrued, product

    accrued, product = doubled(accrued, product, lane, owned, 1)
    heads = jnp.broadcast_to(accrued[:, :1], (peers, owned))
    rates = jnp.broadcast_to(product[:, :1], (peers, owned))
    heads = doubled(heads, rates, line, peers, 0)[0]
    incoming = jnp.where(line < peers - 1, pltpu.roll(heads, peers - 1, 0), 0.0)
    advantage_ref[...] = accrued + product * incoming
    here = lax.axis_index("batch")
    logprob_out[...] = logprob_ref[pl.ds(here, 1), :]
    advantage_out[...] = advantage_ref[pl.ds(here, 1), :]


def finish(grid, parts, rows):
    owned = rows[0].shape[1]
    tokens = owned * CORES
    shape = jax.ShapeDtypeStruct((3 * grid.planes + len(rows), tokens), jnp.float32)
    plane = [
        grid.across(parts, down, along)
        for down in range(grid.side)
        for along in range(grid.side)
        if down or along
    ]
    packed = gather_call(lambda *refs: pack_kernel(grid, *refs), [parts, *plane, *rows], shape, [])
    paired = gather_call(
        lambda *refs: pair_kernel(grid, *refs), [packed, grid.twin(packed)], shape, []
    )
    row = jax.ShapeDtypeStruct((1, owned), jnp.float32)
    planes = [paired] + [grid.up(paired, step) for step in range(1, grid.planes)]
    logprob, advantages = gather_call(
        lambda *refs: tail_kernel(grid, *refs),
        planes,
        (row, row),
        [
            pltpu.VMEM((grid.peers + 1, len(rows), owned), jnp.float32),
            pltpu.VMEM((grid.peers, owned), jnp.float32),
            pltpu.VMEM((grid.peers, owned), jnp.float32),
        ],
    )
    return logprob[0], advantages[0]


def per_device(
    grid, hidden, exit_layer, exit_gains, unembed, targets, values, rewards, ref_logprob, segment_end
):
    owned, _ = hidden.shape
    half_rows = owned // 2
    held = normalize(grid, True, hidden, exit_layer[None], exit_gains)
    hidden, held = lax.optimization_barrier((hidden, held))
    normed = normalize(grid, False, hidden, exit_layer[None], exit_gains)
    ids = targets.reshape(grid.planes, 1, CORES * owned)
    weights = pl.pallas_call(
        load_kernel,
        out_shape=pltpu.VMEM(unembed.T.shape, unembed.dtype),
        in_specs=[ANY],
        out_specs=VMEM,
        scratch_shapes=[pltpu.SemaphoreType.DMA],
        compiler_params=pltpu.CompilerParams(vmem_limit_bytes=2 * MIB),
        name="load",
    )(unembed.T)
    parts = None
    twin = grid.twin(normed)
    above = grid.up(held)
    other = None
    for step in range(grid.planes):
        if step == 0:
            pieces = [
                (lambda core, half: core * owned, normed),
                (lambda core, half: (1 - core) * owned, twin),
            ]
            ahead, weights = lax.optimization_barrier((above, weights))
        else:
            other, parts = lax.optimization_barrier((other, parts))
            pieces = [
                (lambda core, half: core * owned + half * half_rows, held),
                (lambda core, half: core * owned + (1 - half) * half_rows, other),
                (lambda core, half: (1 - core) * owned + half * half_rows, twin),
                (lambda core, half: (1 - core) * owned + (1 - half) * half_rows, grid.twin(other)),
            ]
            if step + 1 < grid.planes:
                ahead, parts = lax.optimization_barrier((above, parts))
        if step + 1 < grid.planes:
            held = ahead
            other = grid.along_y(held) if step % 2 else grid.along_x(held)
            twin = grid.twin(held)
            if step + 2 < grid.planes:
                above = grid.up(held)
        result = score(grid, step, pieces, ids, weights, parts, step == 0)
        parts = result
    rows = [row[None] for row in (values, rewards, ref_logprob, segment_end)]
    return finish(grid, parts, rows)


def solution(mesh):
    grid = Grid(mesh)
    placed = (
        P("batch", None),
        P("batch"),
        P(),
        P(None, ("batch", "vocab")),
        P(),
        P("batch"),
        P("batch"),
        P("batch"),
        P("batch"),
    )

    def body(*arrays):
        return per_device(grid, *arrays)

    return jax.shard_map(
        body,
        mesh=mesh,
        in_specs=placed,
        out_specs=(P("batch"), P("batch")),
        check_vma=False,
    )
```

```python
import math

import jax
import jax.numpy as jnp
from jax import lax
from jax.experimental import pallas as pl
from jax.experimental.pallas import tpu as pltpu
from jax.sharding import PartitionSpec as P


epsilon_norm = 1e-05
discount = 1.0
trace_decay = 0.999
penalty_weight = 0.1
CORES = 2
LOWEST = float(jnp.finfo(jnp.float32).min)
VMEM = pl.BlockSpec(memory_space=pltpu.VMEM)
ANY = pl.BlockSpec(memory_space=pl.ANY)
HBM = pl.BlockSpec(memory_space=pltpu.HBM)
MIB = 2**20


class Grid:
    def __init__(self, mesh):
        self.peers, self.groups = mesh.shape["batch"], mesh.shape["vocab"]
        self.planes = self.peers // CORES
        self.side = math.isqrt(self.groups)

    def moves(self, target):
        pairs = []
        for b in range(self.peers):
            for v in range(self.groups):
                z, c, y, x = target(b // CORES, b % CORES, v // self.side, v % self.side)
                pairs.append((b * self.groups + v, (z * CORES + c) * self.groups + y * self.side + x))
        return pairs

    def send(self, array, target):
        return lax.ppermute(array, ("batch", "vocab"), self.moves(target))

    def twin(self, array):
        return self.send(array, lambda z, c, y, x: (z, 1 - c, y, x))

    def line(self, position):
        position %= self.planes
        return 2 * position - 1 if 0 < 2 * position <= self.planes else 2 * (self.planes - position) % self.planes

    def up(self, array, steps=1):
        where = {self.line(position): position for position in range(self.planes)}
        return self.send(array, lambda z, c, y, x: (self.line(where[z] + steps), c, y, x))

    def origin(self, plane, steps):
        if steps == 0:
            return plane
        count = self.planes
        even = lax.rem(count - lax.div(plane, 2), count)
        position = jnp.where(lax.rem(plane, 2) == 1, lax.div(plane + 1, 2), even)
        position = lax.rem(position - steps + count, count)
        low = (position > 0) & (2 * position <= count)
        return jnp.where(low, 2 * position - 1, lax.rem(2 * (count - position), count))

    def across(self, array, down, along):
        side = self.side
        return self.send(array, lambda z, c, y, x: (z, c, (y + down) % side, (x + along) % side))

    def along_x(self, array):
        return self.send(array, lambda z, c, y, x: (z, c, y, x ^ 1))

    def along_y(self, array):
        return self.send(array, lambda z, c, y, x: (z, c, y ^ 1, x))

    def place(self):
        b, v = lax.axis_index("batch"), lax.axis_index("vocab")
        half = lax.rem(lax.div(v, self.side) + lax.rem(v, self.side), 2)
        return lax.div(b, CORES), lax.rem(b, CORES), half


def normalize_kernel(grid, halved, hidden_hbm, layers_hbm, gains_hbm, out_ref,
                     states_ref, layers_ref, wide_ref, gains_ref, sem):
    rows = out_ref.shape[0]
    block = 16
    chunk = 32
    exits = gains_ref.shape[0]
    half = grid.place()[2]
    start = pl.multiple_of((half if halved else 1 - half) * rows, rows)
    small = [
        pltpu.make_async_copy(layers_hbm, layers_ref, sem.at[0]),
        pltpu.make_async_copy(gains_hbm, gains_ref, sem.at[1]),
    ]
    large = []
    for index in range(rows // chunk):
        large.append(
            pltpu.make_async_copy(
                hidden_hbm.at[pl.ds(start + index * chunk, chunk)],
                states_ref.at[pl.ds(index * chunk, chunk)],
                sem.at[2 + index],
            )
        )
    for copy in small + large:
        copy.start()
    small[0].wait()
    owned = layers_ref.shape[1]
    wide_ref[...] = jnp.broadcast_to(layers_ref[...], (owned, owned)).astype(jnp.float32).T
    small[1].wait()
    for index, copy in enumerate(large):
        copy.wait()

        def body(turn, carry):
            begin = pl.multiple_of(index * chunk + turn * block, block)
            part = pl.ds(begin, block)
            states = states_ref[part, :].astype(jnp.float32)
            mean = jnp.sum(states * states, axis=1, keepdims=True) / states.shape[1]
            inverse = lax.rsqrt(mean + epsilon_norm)
            layer = wide_ref[pl.ds(pl.multiple_of(start + begin, block), block), :1]
            scaling = jnp.broadcast_to(gains_ref[0:1, :], states.shape)
            for exit_index in range(1, exits):
                scaling = jnp.where(
                    layer == float(exit_index), gains_ref[exit_index : exit_index + 1, :], scaling
                )
            out_ref[part, :] = (states * inverse * scaling).astype(out_ref.dtype)
            return carry

        lax.fori_loop(0, chunk // block, body, 0)


def normalize(grid, halved, hidden, layers, gains):
    owned, width = hidden.shape
    rows = owned // 2
    return pl.pallas_call(
        lambda *refs: normalize_kernel(grid, halved, *refs),
        out_shape=jax.ShapeDtypeStruct((rows, width), jnp.bfloat16),
        in_specs=[HBM] * 3,
        out_specs=VMEM,
        scratch_shapes=[
            pltpu.VMEM((rows, width), hidden.dtype),
            pltpu.VMEM(layers.shape, layers.dtype),
            pltpu.VMEM((owned, owned), jnp.float32),
            pltpu.VMEM(gains.shape, gains.dtype),
            pltpu.SemaphoreType.DMA((2 + rows // 32,)),
        ],
        compiler_params=pltpu.CompilerParams(vmem_limit_bytes=60 * MIB),
        name="share" if halved else "normalize",
    )(hidden, layers, gains)


def spans(rows, target):
    count = max(1, round(rows / target))
    size = -(-rows // (count * 16)) * 16
    return [(begin, min(size, rows - begin)) for begin in range(0, rows, size)]


def tally(logits, begin, wanted, carry):
    old, total, pick = carry
    place = lax.broadcasted_iota(jnp.int32, logits.shape, 0) + begin
    new = jnp.maximum(old, jnp.max(logits, axis=0, keepdims=True))
    total = total * jnp.exp(old - new) + jnp.sum(jnp.exp(logits - new), axis=0, keepdims=True)
    pick = pick + jnp.sum(jnp.where(place == wanted, logits, 0.0), axis=0, keepdims=True)
    return new, total, pick


def product(weights, states):
    return lax.dot_general(
        weights, states, (((1,), (1,)), ((), ())), preferred_element_type=jnp.float32
    )


def score_kernel(grid, step, pieces, first, *refs):
    refs = list(refs)
    ids_ref, weights_in = refs.pop(0), refs.pop(0)
    parts_in = None if first else refs.pop(0)
    piece_refs = [refs.pop(0) for _ in pieces]
    parts_ref = refs.pop(0)
    weights_ref = weights_in
    states_ref, piece_sem = refs.pop(0), refs.pop(0)
    rows = weights_ref.shape[0]
    plane, core, half = grid.place()
    source = grid.origin(plane, step)
    copies = []
    for index, (piece, ref) in enumerate(zip(pieces, piece_refs)):
        offset = pl.multiple_of(piece(core, half), ref.shape[0])
        copies.append(
            pltpu.make_async_copy(ref, states_ref.at[pl.ds(offset, ref.shape[0])], piece_sem.at[index])
        )
    for copy in copies:
        copy.start()
    blocks = spans(rows, 1336)
    for copy in copies:
        copy.wait()
    start = (lax.axis_index("batch") * grid.groups + lax.axis_index("vocab")) * rows
    wanted = ids_ref[source] - start
    tokens = states_ref.shape[0]
    carry = (
        jnp.full((1, tokens), LOWEST, jnp.float32),
        jnp.zeros((1, tokens), jnp.float32),
        jnp.zeros((1, tokens), jnp.float32),
    )
    pending = None
    for begin, size in blocks:
        logits = product(weights_ref[begin : begin + size, :], states_ref[...])
        if pending is not None:
            carry = tally(*pending, wanted, carry)
        pending = (logits, begin)
    carry = tally(*pending, wanted, carry)
    if not first:
        parts_ref[...] = parts_in[...]
    for index in range(3):
        parts_ref[source, index : index + 1, :] = carry[index]


def score(grid, step, pieces, ids, weights, parts, first):
    owned = pieces[0][1].shape[0] * 2
    width = weights.shape[1]
    rows = weights.shape[0]
    tokens = owned * CORES
    out_shape = jax.ShapeDtypeStruct((grid.planes, 3, tokens), jnp.float32)
    args = [ids, weights]
    specs = [VMEM, VMEM]
    if not first:
        args.append(parts)
        specs.append(VMEM)
    args += [array for _, array in pieces]
    specs += [HBM] * len(pieces)
    scratch = [
        pltpu.VMEM((tokens, width), jnp.bfloat16),
        pltpu.SemaphoreType.DMA((len(pieces),)),
    ]
    out_specs = VMEM
    limit = 8
    offsets = [offset for offset, _ in pieces]
    return pl.pallas_call(
        lambda *refs: score_kernel(grid, step, offsets, first, *refs),
        out_shape=out_shape,
        in_specs=specs,
        out_specs=out_specs,
        scratch_shapes=scratch,
        compiler_params=pltpu.CompilerParams(vmem_limit_bytes=limit * MIB),
        cost_estimate=pl.CostEstimate(
            flops=2 * rows * tokens * width, transcendentals=rows * tokens, bytes_accessed=0
        ),
    )(*args)


def load_kernel(weights_in, weights_ref, sem):
    copy = pltpu.make_async_copy(weights_in, weights_ref, sem)
    copy.start()
    copy.wait()


def joined(sources):
    larger = sources[0][0]
    for source in sources[1:]:
        larger = jnp.maximum(larger, source[0])
    total = sum(source[1] * jnp.exp(source[0] - larger) for source in sources)
    return larger, total, sum(source[2] for source in sources)


def triple(ref, count):
    return [ref[index * count : (index + 1) * count, :] for index in range(3)]


def brought(kernel, count):
    def body(*refs):
        held, sem = refs[len(refs) - count - 1 : -1], refs[-1]
        copies = [
            pltpu.make_async_copy(ref, to, sem.at[index])
            for index, (ref, to) in enumerate(zip(refs[:count], held))
        ]
        for copy in copies:
            copy.start()
        for copy in copies:
            copy.wait()
        kernel(*held, *refs[count : len(refs) - count - 1])

    return body


def gather_call(kernel, arrays, out_shape, scratch):
    many = isinstance(out_shape, tuple)
    held = [pltpu.VMEM(array.shape, array.dtype) for array in arrays]
    return pl.pallas_call(
        brought(kernel, len(arrays)),
        out_shape=out_shape,
        in_specs=[ANY] * len(arrays),
        out_specs=(VMEM,) * len(out_shape) if many else VMEM,
        scratch_shapes=scratch + held + [pltpu.SemaphoreType.DMA((len(arrays),))],
        compiler_params=pltpu.CompilerParams(vmem_limit_bytes=4 * MIB),
    )(*arrays)


def pack_kernel(grid, *refs):
    parts, rows, out_ref = refs[: grid.groups], refs[grid.groups : -1], refs[-1]
    count = grid.planes
    merged = joined([[ref[:, index, :] for index in range(3)] for ref in parts])
    for index in range(3):
        out_ref[index * count : (index + 1) * count, :] = merged[index]
    tokens = out_ref.shape[1]
    owned = tokens // CORES
    core = grid.place()[1]
    lane = lax.broadcasted_iota(jnp.int32, (1, tokens), 1)
    mine = (lane >= core * owned) & (lane < core * owned + owned)
    for index, ref in enumerate(rows):
        row = ref[...].astype(jnp.float32)
        row = jnp.concatenate([row] * CORES, axis=1)
        out_ref[3 * count + index : 3 * count + index + 1, :] = jnp.where(mine, row, 0.0)


def pair_kernel(grid, mine_ref, other_ref, out_ref):
    count = grid.planes
    merged = joined([triple(mine_ref, count), triple(other_ref, count)])
    for index in range(3):
        out_ref[index * count : (index + 1) * count, :] = merged[index]
    out_ref[3 * count :, :] = mine_ref[3 * count :, :] + other_ref[3 * count :, :]


def tail_kernel(grid, *refs):
    count = grid.planes
    sources = refs[:count]
    logprob_out, advantage_out, rows_ref, logprob_ref, advantage_ref = refs[count:]
    peers, owned = logprob_ref.shape
    plane = grid.place()[0]
    larger, total, picked = joined([triple(ref, count) for ref in sources])
    logprob = picked - (larger + jnp.log(total))
    for group in range(count):
        for core in range(CORES):
            span = slice(core * owned, (core + 1) * owned)
            row = group * CORES + core
            logprob_ref[row : row + 1, :] = logprob[group : group + 1, span]
    for step, ref in enumerate(sources):
        source = grid.origin(plane, step)
        for core in range(CORES):
            span = slice(core * owned, (core + 1) * owned)
            rows_ref[source * CORES + core] = ref[3 * count :, span]
    rows_ref[peers] = jnp.zeros(rows_ref.shape[1:], jnp.float32)
    lane = lax.broadcasted_iota(jnp.int32, (peers, owned), 1)
    line = lax.broadcasted_iota(jnp.int32, (peers, owned), 0)
    logprob = logprob_ref[...]
    values = rows_ref[0:peers, 0, :]
    entering = jnp.broadcast_to(rows_ref[1 : peers + 1, 0, :][:, :1], (peers, owned))
    following = jnp.where(lane < owned - 1, pltpu.roll(values, owned - 1, 1), entering)
    keeping = 1.0 - rows_ref[0:peers, 3, :]
    shaped = rows_ref[0:peers, 1, :] - penalty_weight * (logprob - rows_ref[0:peers, 2, :])
    accrued = shaped + discount * following * keeping - values
    product = discount * trace_decay * keeping

    def doubled(accrued, product, place, extent, axis):
        steps = 1
        while steps < extent:
            inside = place < extent - steps
            later = jnp.where(inside, pltpu.roll(accrued, extent - steps, axis), 0.0)
            accrued = accrued + product * later
            product = product * jnp.where(inside, pltpu.roll(product, extent - steps, axis), 1.0)
            steps *= 2
        return accrued, product

    accrued, product = doubled(accrued, product, lane, owned, 1)
    heads = jnp.broadcast_to(accrued[:, :1], (peers, owned))
    rates = jnp.broadcast_to(product[:, :1], (peers, owned))
    heads = doubled(heads, rates, line, peers, 0)[0]
    incoming = jnp.where(line < peers - 1, pltpu.roll(heads, peers - 1, 0), 0.0)
    advantage_ref[...] = accrued + product * incoming
    here = lax.axis_index("batch")
    logprob_out[...] = logprob_ref[pl.ds(here, 1), :]
    advantage_out[...] = advantage_ref[pl.ds(here, 1), :]


def finish(grid, parts, rows):
    owned = rows[0].shape[1]
    tokens = owned * CORES
    shape = jax.ShapeDtypeStruct((3 * grid.planes + len(rows), tokens), jnp.float32)
    plane = [
        grid.across(parts, down, along)
        for down in range(grid.side)
        for along in range(grid.side)
        if down or along
    ]
    packed = gather_call(lambda *refs: pack_kernel(grid, *refs), [parts, *plane, *rows], shape, [])
    paired = gather_call(
        lambda *refs: pair_kernel(grid, *refs), [packed, grid.twin(packed)], shape, []
    )
    row = jax.ShapeDtypeStruct((1, owned), jnp.float32)
    planes = [paired] + [grid.up(paired, step) for step in range(1, grid.planes)]
    logprob, advantages = gather_call(
        lambda *refs: tail_kernel(grid, *refs),
        planes,
        (row, row),
        [
            pltpu.VMEM((grid.peers + 1, len(rows), owned), jnp.float32),
            pltpu.VMEM((grid.peers, owned), jnp.float32),
            pltpu.VMEM((grid.peers, owned), jnp.float32),
        ],
    )
    return logprob[0], advantages[0]


def per_device(
    grid, hidden, exit_layer, exit_gains, unembed, targets, values, rewards, ref_logprob, segment_end
):
    owned, _ = hidden.shape
    half_rows = owned // 2
    held = normalize(grid, True, hidden, exit_layer[None], exit_gains)
    hidden, held = lax.optimization_barrier((hidden, held))
    normed = normalize(grid, False, hidden, exit_layer[None], exit_gains)
    ids = targets.reshape(grid.planes, 1, CORES * owned)
    weights = pl.pallas_call(
        load_kernel,
        out_shape=pltpu.VMEM(unembed.T.shape, unembed.dtype),
        in_specs=[ANY],
        out_specs=VMEM,
        scratch_shapes=[pltpu.SemaphoreType.DMA],
        compiler_params=pltpu.CompilerParams(vmem_limit_bytes=2 * MIB),
        name="load",
    )(unembed.T)
    parts = None
    twin = grid.twin(held)
    above = grid.up(held)
    other = None
    for step in range(grid.planes):
        if step == 0:
            pieces = [
                (lambda core, half: core * owned + half * half_rows, held),
                (lambda core, half: core * owned + (1 - half) * half_rows, normed),
                (lambda core, half: (1 - core) * owned + half * half_rows, twin),
                (lambda core, half: (1 - core) * owned + (1 - half) * half_rows, grid.twin(normed)),
            ]
            ahead, weights = lax.optimization_barrier((above, weights))
        else:
            other, parts = lax.optimization_barrier((other, parts))
            pieces = [
                (lambda core, half: core * owned + half * half_rows, held),
                (lambda core, half: core * owned + (1 - half) * half_rows, other),
                (lambda core, half: (1 - core) * owned + half * half_rows, twin),
                (lambda core, half: (1 - core) * owned + (1 - half) * half_rows, grid.twin(other)),
            ]
            if step + 1 < grid.planes:
                ahead, parts = lax.optimization_barrier((above, parts))
        if step + 1 < grid.planes:
            held = ahead
            other = grid.along_y(held) if step % 2 else grid.along_x(held)
            twin = grid.twin(held)
            if step + 2 < grid.planes:
                above = grid.up(held)
        result = score(grid, step, pieces, ids, weights, parts, step == 0)
        parts = result
    rows = [row[None] for row in (values, rewards, ref_logprob, segment_end)]
    return finish(grid, parts, rows)


def solution(mesh):
    grid = Grid(mesh)
    placed = (
        P("batch", None),
        P("batch"),
        P(),
        P(None, ("batch", "vocab")),
        P(),
        P("batch"),
        P("batch"),
        P("batch"),
        P("batch"),
    )

    def body(*arrays):
        return per_device(grid, *arrays)

    return jax.shard_map(
        body,
        mesh=mesh,
        in_specs=placed,
        out_specs=(P("batch"), P("batch")),
        check_vma=False,
    )
```
